32 devices in a mesh: dp: 4 (over y, x), expert: 8 (over z, core).
Axes of the slice: x: 2, y: 2, z: 4, core: 2. Of those that a mesh axis runs over, the one named last changes fastest.
Arguments:
- tokens: bfloat16 [192, 4096], P('expert', 'dp'), may hold values from -6 to 6
- expert_ids: int32 [192, 8], P('expert'), may hold values from 0 to 15, as said below
- router_probs: float32 [192, 8], P('expert'), may hold values from 0.05 to 1
- w_gate: bfloat16 [16, 4096, 768], P('expert', 'dp'), may hold values from -0.09375 to 0.09375
- w_up: bfloat16 [16, 4096, 768], P('expert', 'dp'), may hold values from -0.09375 to 0.09375
- w_down: bfloat16 [16, 768, 4096], P('expert', None, 'dp'), may hold values from -0.21875 to 0.21875
Outputs:
- mixed: bfloat16 [192, 4096], P('expert', 'dp')
The draws below stay inside these ranges and needn't reach their ends.
Inputs may be any that keep to these rules, and one draw needn't show every extreme that they name: `expert_ids`: each token names 8 different experts. Call hot the two experts named by the most rows over all tokens: in each aligned block of 24 rows (the rows of one device) each of them is named by more than 15 rows, every other expert by at most 15 rows, and some other expert by exactly 15 rows in every block.
All inputs are finite; a program needn't handle non-finite values.
Results may differ from the reference program's by a relative error of at most 0.0058.
Values may be sent and summed in bfloat16 or wider, within the bound.
A program may use at most 128 MiB of HBM per device.

```python
import math
import jax
import jax.numpy as jnp
from jax import lax

D = 4096
TOP = 8
FFW = 768
TOK_DEV = 24
EXPERTS = 16
TOKENS = 192
CAP = 15
N_EXPERT = 8


def draw_expert_ids(key, part):
    base = jax.random.fold_in(key, 7)
    key_pick, key_rows, key_flags, key_order = jax.random.split(base, 4)
    picked = jax.random.permutation(key_pick, EXPERTS).astype(jnp.int32)
    hot_pair = picked[:2]
    full_expert = picked[2]
    pool = picked[3:]
    pool_size = EXPERTS - 3
    blocks = TOKENS // TOK_DEV
    rank_first = jax.vmap(lambda row_key: jax.random.permutation(row_key, TOK_DEV))(jax.random.split(jax.random.fold_in(key_flags, 3), blocks))
    rank_second = jax.vmap(lambda row_key: jax.random.permutation(row_key, TOK_DEV))(jax.random.split(jax.random.fold_in(key_flags, 4), blocks))
    flag_first = ((jax.random.randint(jax.random.fold_in(key_flags, 1), (blocks, TOK_DEV), 0, 10) < 3) | (rank_first < CAP + 1)).astype(jnp.int32)
    flag_second = ((jax.random.randint(jax.random.fold_in(key_flags, 2), (blocks, TOK_DEV), 0, 10) < 2) | (rank_second < CAP + 1)).astype(jnp.int32)
    with_full = (jnp.arange(TOK_DEV) < CAP).astype(jnp.int32)[None, :]
    fixed_count = flag_first + flag_second + with_full
    pool_count = TOP - fixed_count
    pool_start = jnp.cumsum(pool_count, axis=1) - pool_count
    block_keys = jax.random.split(key_rows, blocks)
    block_pools = jax.vmap(lambda row_key: pool[jax.random.permutation(row_key, pool_size)])(block_keys)
    column = jnp.arange(TOP, dtype=jnp.int32)[None, None, :]
    offset = (pool_start[:, :, None] + column - fixed_count[:, :, None]) % pool_size
    from_pool = jnp.take_along_axis(block_pools, offset.reshape(blocks, TOK_DEV * TOP), axis=1).reshape(blocks, TOK_DEV, TOP)
    first_edge = flag_first[:, :, None]
    second_edge = (flag_first + flag_second)[:, :, None]
    named = jnp.where(column < first_edge, hot_pair[0], jnp.where(column < second_edge, hot_pair[1], jnp.where(column < fixed_count[:, :, None], full_expert, from_pool)))
    named = named.reshape(TOKENS, TOP).astype(jnp.int32)
    row_keys = jax.random.split(key_order, TOKENS)
    shuffled = jax.vmap(lambda row_key, row_ids: row_ids[jax.random.permutation(row_key, TOP)])(row_keys, named)
    return shuffled.astype(jnp.int32)


def block_levels(key, shape, cuts, smallest, largest):
    gain = 1.0
    for position, parts in cuts:
        draws = jax.random.uniform(jax.random.fold_in(jax.random.fold_in(key, 6), position), (parts,), jnp.float32, smallest / len(cuts), largest / len(cuts))
        gain = gain * jnp.repeat(jnp.exp(draws), shape[position] // parts).reshape((-1,) + (1,) * (len(shape) - 1 - position))
    return gain


def scatter_about(key, shape, deviation, most, cuts=(), kind=jnp.bfloat16):
    values = jax.random.normal(key, shape, jnp.float32) * deviation
    if len(cuts) > 0:
        values = block_levels(key, shape, cuts, -0.22, 0.18) * values
    return jnp.clip(values, min=-most, max=most).astype(kind)


def setup_inputs(seed: int = 0) -> dict:
    key_of = jax.random.split(jax.random.key(seed), 7)
    return {
        "tokens": scatter_about(key_of[0], (TOKENS, D), 1.0, 6.0, ((0, 8), (1, 4))),
        "expert_ids": draw_expert_ids(jax.random.fold_in(key_of[6], 71), 0),
        "router_probs": jnp.clip(jnp.exp(math.log(1.0) - 2.9957323 * jax.random.uniform(key_of[2], (TOKENS, TOP), jnp.float32) ** block_levels(key_of[2], (TOKENS, TOP), ((0, 8),), -0.2, 0.2)), 0.05, 1.0),
        "w_gate": scatter_about(key_of[3], (EXPERTS, D, FFW), D ** -0.5, 0.09375, ((0, 8), (1, 4))),
        "w_up": scatter_about(key_of[4], (EXPERTS, D, FFW), D ** -0.5, 0.09375, ((0, 8), (1, 4))),
        "w_down": scatter_about(key_of[5], (EXPERTS, FFW, D), FFW ** -0.5, 0.21875, ((0, 8), (2, 4))),
    }


def expert_rows(rows, gate_w, up_w, down_w):
    gate = jnp.dot(rows, gate_w, preferred_element_type=jnp.float32)
    up_val = jnp.dot(rows, up_w, preferred_element_type=jnp.float32)
    hidden = (jax.nn.silu(gate) * up_val).astype(jnp.bfloat16)
    return jnp.dot(hidden, down_w, preferred_element_type=jnp.float32).astype(jnp.bfloat16)


def reference(tokens, expert_ids, router_probs, w_gate, w_up, w_down):
    weights = router_probs / jnp.sum(router_probs, axis=1, keepdims=True)
    flat_ids = expert_ids.reshape(-1).astype(jnp.int32)
    every_expert = jnp.arange(EXPERTS, dtype=jnp.int32)
    name_counts = jnp.sum((flat_ids[:, None] == every_expert[None, :]).astype(jnp.int32), axis=0).astype(jnp.int32)
    first_hot = jnp.argmax(name_counts).astype(jnp.int32)
    second_hot = jnp.argmax(jnp.where(every_expert == first_hot, -1, name_counts)).astype(jnp.int32)
    hot_ids = jnp.stack([first_hot, second_hot]).astype(jnp.int32)
    flat_weights = weights.reshape(-1)
    owners = (jnp.arange(TOKENS * TOP, dtype=jnp.int32) // TOP).astype(jnp.int32)
    is_hot = (flat_ids == hot_ids[0]) | (flat_ids == hot_ids[1])
    sort_key = jnp.where(is_hot, EXPERTS, flat_ids).astype(jnp.int32)
    order = jnp.argsort(sort_key, stable=True)
    counts = jnp.sum((sort_key[:, None] == every_expert[None, :]).astype(jnp.int32), axis=0).astype(jnp.int32)
    starts = (jnp.cumsum(counts) - counts).astype(jnp.int32)
    span = N_EXPERT * CAP
    sorted_rows = jnp.concatenate([owners[order], jnp.zeros((span,), jnp.int32)]).astype(jnp.int32)
    sorted_weights = jnp.concatenate([flat_weights[order], jnp.zeros((span,), jnp.float32)])
    live_index = jnp.arange(span, dtype=jnp.int32)

    def visit(total, expert):
        begin = starts[expert]
        rows = lax.dynamic_slice_in_dim(sorted_rows, begin, span).astype(jnp.int32)
        scale = lax.dynamic_slice_in_dim(sorted_weights, begin, span)
        scale = jnp.where(live_index < counts[expert], scale, jnp.zeros_like(scale))
        result = expert_rows(tokens[rows], w_gate[expert], w_up[expert], w_down[expert])
        total = total.at[rows].add(scale[:, None] * result.astype(jnp.float32))
        return total, None

    total, _ = lax.scan(visit, jnp.zeros((TOKENS, D), jnp.float32), every_expert)
    for slot in range(2):
        chosen = hot_ids[slot]
        hot_weight = jnp.sum(jnp.where(expert_ids == chosen, weights, jnp.zeros_like(weights)), axis=1)
        result = expert_rows(tokens, w_gate[chosen], w_up[chosen], w_down[chosen])
        total = total + hot_weight[:, None] * result.astype(jnp.float32)
    return total.astype(jnp.bfloat16)
```

```python
import functools

import jax
import jax.numpy as jnp
from jax import lax
from jax.experimental import pallas as pl
from jax.experimental.pallas import tpu as pltpu
from jax.sharding import PartitionSpec as P

MESH = pl.DeviceIdType.MESH
F32, BF16 = jnp.float32, jnp.bfloat16


def from_root(x, axis, root):
    mine = lax.axis_index(axis) == root
    return lax.psum(jnp.where(mine, x, jnp.zeros_like(x)), axis)


def shards(tokens, expert_ids, router_probs, w_gate, w_up, w_down):
    tok_rows, width_part = tokens.shape
    top_count = expert_ids.shape[1]
    local_experts = w_gate.shape[0]
    groups = lax.axis_size("expert")
    experts_all = local_experts * groups
    capacity = max(2, (tok_rows * top_count + experts_all - 4) // (experts_all - 3))
    slots_all = experts_all * capacity
    weights = router_probs / jnp.sum(router_probs, axis=1, keepdims=True)
    flat_ids = expert_ids.reshape(-1)
    every_expert = jnp.arange(experts_all, dtype=jnp.int32)
    named_table = (flat_ids[:, None] == every_expert[None, :]).astype(jnp.int32)
    local_counts = jnp.sum(named_table, axis=0)
    above_cap = (local_counts > capacity).astype(jnp.int32)
    first_hot = jnp.argmax(above_cap)
    second_hot = experts_all - 1 - jnp.argmax(above_cap[::-1])
    hot_ids = jnp.stack([first_hot, second_hot])
    is_hot = (expert_ids == hot_ids[0]) | (expert_ids == hot_ids[1])
    cold_mask = jnp.logical_not(is_hot).reshape(-1)
    member = named_table * cold_mask[:, None].astype(jnp.int32)
    row = jnp.arange(member.shape[0], dtype=jnp.int32)
    before = (row[:, None] > row[None, :]).astype(jnp.bfloat16)
    earlier = jnp.dot(before, member.astype(jnp.bfloat16), preferred_element_type=jnp.float32)
    position = jnp.sum(earlier.astype(jnp.int32) * member, axis=1)
    slot_index = jnp.where(cold_mask, flat_ids * capacity + position, -1)
    matches = (slot_index[:, None] == jnp.arange(slots_all, dtype=jnp.int32)[None, :]).reshape(
        tok_rows, top_count, slots_all
    )
    chosen = jnp.sum(matches.astype(jnp.bfloat16), axis=1)
    combine_mat = jnp.sum(jnp.where(matches, weights[:, :, None], 0.0), axis=1)
    outgoing = jnp.einsum("ts,td->sd", chosen, tokens, preferred_element_type=jnp.float32).astype(
        jnp.bfloat16
    )
    outgoing = outgoing.reshape(groups, local_experts, capacity, width_part)
    received = lax.all_to_all(outgoing, "expert", split_axis=0, concat_axis=0, tiled=True)
    gate_part = jnp.einsum("secd,edf->escf", received, w_gate, preferred_element_type=jnp.float32)
    up_part = jnp.einsum("secd,edf->escf", received, w_up, preferred_element_type=jnp.float32)
    gate_sum, up_sum = lax.psum((gate_part, up_part), "dp")
    hidden = (jax.nn.silu(gate_sum) * up_sum).astype(jnp.bfloat16)
    output = jnp.einsum("escf,efd->secd", hidden, w_down, preferred_element_type=jnp.float32)
    results = output.astype(jnp.bfloat16)
    returned = lax.all_to_all(results, "expert", split_axis=0, concat_axis=0, tiled=True)
    main_part = jnp.dot(
        combine_mat,
        returned.reshape(slots_all, width_part).astype(jnp.float32),
        precision=lax.Precision.HIGHEST,
    )
    hot_gates = []
    hot_ups = []
    hot_downs = []
    for hot_slot in range(2):
        hot_expert = hot_ids[hot_slot]
        root_index = hot_expert // local_experts
        local_index = hot_expert % local_experts
        pieces = (
            lax.dynamic_index_in_dim(w_gate, local_index, 0, keepdims=False),
            lax.dynamic_index_in_dim(w_up, local_index, 0, keepdims=False),
            lax.dynamic_index_in_dim(w_down, local_index, 0, keepdims=False),
        )
        gate_copy, up_copy, down_copy = (
            from_root(pieces[0], "expert", root_index),
            from_root(pieces[1], "expert", root_index),
            from_root(pieces[2], "expert", root_index),
        )
        hot_gates.append(jnp.dot(tokens, gate_copy, preferred_element_type=jnp.float32))
        hot_ups.append(jnp.dot(tokens, up_copy, preferred_element_type=jnp.float32))
        hot_downs.append(down_copy)
    gate_total, up_total = lax.psum((jnp.stack(hot_gates), jnp.stack(hot_ups)), "dp")
    hot_hidden = (jax.nn.silu(gate_total) * up_total).astype(jnp.bfloat16)
    total = main_part
    for hot_slot in range(2):
        hot_out = jnp.dot(
            hot_hidden[hot_slot], hot_downs[hot_slot], preferred_element_type=jnp.float32
        ).astype(jnp.bfloat16)
        hot_weight = jnp.sum(jnp.where(expert_ids == hot_ids[hot_slot], weights, 0.0), axis=1)
        total = total + hot_weight[:, None] * hot_out.astype(jnp.float32)
    return total.astype(jnp.bfloat16)


def rows_of(blocks):
    count, rows, width = blocks.shape
    return blocks.astype(F32).reshape(count * rows, width).astype(BF16)


def kernel(
    tokens_hbm, ids_hbm, probs_hbm, gate_hbm, up_hbm, down_hbm, out_ref,
    tokens_ref, ids_ref, probs_ref, wg, wu, wd, tok, mix, part, leave, got, hid, outp, pout, pair, zsend, zgot,
    in_sem, w_sem, tok_send, tok_recv, fwd_send, fwd_recv, mix_send, mix_recv, mix_fwd_send, mix_fwd_recv,
    part_send, part_recv, hid_send, hid_recv, pair_send, pair_recv, z_send, z_recv,
):
    local, _, ffw = wg.shape
    rows = tokens_ref.shape[0]
    dp = lax.axis_index("dp")
    me = lax.axis_index("expert")
    z, core = me // 2, me % 2
    low, high = z % 2, z // 2
    zx = (z, z + 1 - 2 * low, z + 2 - 4 * high, 3 - z)
    dlow, dhigh = dp % 2, dp // 2
    dx = (dp, dp + 1 - 2 * dlow, dp + 2 - 4 * dhigh, 3 - dp)
    other = 1 - core
    partner = {"expert": z * 2 + other}

    def send(src, dst, s_sem, r_sem, device):
        copy = pltpu.make_async_remote_copy(
            src_ref=src, dst_ref=dst, send_sem=s_sem, recv_sem=r_sem,
            device_id=device, device_id_type=MESH,
        )
        copy.start()
        sent.append(copy)
        return copy

    barrier = pltpu.get_barrier_semaphore()
    for r in range(1, 3):
        pl.semaphore_signal(barrier, inc=1, device_id={"dp": dx[r]}, device_id_type=MESH)
    for k in range(1, 4):
        pl.semaphore_signal(barrier, inc=1, device_id={"expert": zx[k] * 2 + core}, device_id_type=MESH)
    pl.semaphore_signal(barrier, inc=1, device_id=partner, device_id_type=MESH)

    sent = []
    small = [
        pltpu.make_async_copy(tokens_hbm, tokens_ref, in_sem.at[0]),
        pltpu.make_async_copy(ids_hbm, ids_ref, in_sem.at[1]),
        pltpu.make_async_copy(probs_hbm, probs_ref, in_sem.at[2]),
    ]
    for copy in small:
        copy.start()
    loads = []
    for e in range(local):
        loads.append([
            pltpu.make_async_copy(gate_hbm.at[e], wg.at[e], w_sem.at[3 * e]),
            pltpu.make_async_copy(up_hbm.at[e], wu.at[e], w_sem.at[3 * e + 1]),
            pltpu.make_async_copy(down_hbm.at[e], wd.at[e], w_sem.at[3 * e + 2]),
        ])
    for which in range(3):
        for e in range(local):
            loads[e][which].start()

    def ready(e, which):
        if loads[e][which] is not None:
            loads[e][which].wait()
            loads[e][which] = None

    pl.semaphore_wait(barrier, 6)

    small[0].wait()

    fwd_copies = {}
    fwd_copies[0] = send(tokens_ref, tok.at[z, core], fwd_send.at[0], fwd_recv.at[0], partner)
    tok_copies = {}
    for k in (2, 3, 1):
        tok_copies[k] = send(
            tokens_ref, tok.at[z, core], tok_send.at[k - 1], tok_recv.at[k - 1],
            {"expert": zx[k] * 2 + core},
        )
    tok[z, core] = tokens_ref[...]

    small[1].wait()
    small[2].wait()
    probs = probs_ref[...]
    weights = probs / jnp.sum(probs, axis=0, keepdims=True)
    ids = ids_ref[...]
    named = lax.broadcasted_iota(jnp.int32, mix.shape[2:], 0)
    table = jnp.zeros(mix.shape[2:], F32)
    for k in range(ids.shape[0]):
        table = table + jnp.where(ids[k : k + 1] == named, weights[k : k + 1], 0.0)
    mix[z, core] = table
    mine = mix.at[z, core]
    mix_fwd, mix_copies = {}, {}
    mix_fwd[0] = send(mine, mine, mix_fwd_send.at[0], mix_fwd_recv.at[0], partner)
    for k in (2, 3, 1):
        mix_copies[k] = send(
            mine, mine, mix_send.at[k - 1], mix_recv.at[k - 1], {"expert": zx[k] * 2 + core}
        )

    def pass_on(k):
        tok_copies[k].wait_recv()
        here = tok.at[zx[k], core]
        fwd_copies[k] = send(here, here, fwd_send.at[k], fwd_recv.at[k], partner)

    def pass_mix(k):
        mix_copies[k].wait_recv()
        here = mix.at[zx[k], core]
        mix_fwd[k] = send(here, here, mix_fwd_send.at[k], mix_fwd_recv.at[k], partner)

    part_copies, hid_copies = {}, {}

    def put(k, slot, value):
        leave[k, slot] = value.astype(BF16)
        part_copies[k, slot] = send(
            leave.at[k, slot], got.at[k, slot], part_send.at[k, slot], part_recv.at[k, slot],
            {"dp": dx[1 + slot % 2]},
        )

    def take(k, slot):
        part_copies[k, slot].wait_recv()
        return got[k, slot].astype(F32)

    def up_side(k):
        fwd_copies[k].wait_recv()
        x = rows_of(tok[zx[k]])
        for which, w in ((0, wg), (1, wu)):
            for e in range(local):
                ready(e, which)
                part[k, which, 2 * e : 2 * e + 2] = (
                    jnp.dot(x, w[e], preferred_element_type=F32).reshape(2, rows, ffw)
                )
            put(k, which, part[k, which, dx[3]])
            put(k, which + 2, part[k, which, dx[1 + which]])

    def relay(k):
        put(k, 5, part[k, 0, dx[2]] + take(k, 0))
        put(k, 4, part[k, 1, dx[1]] + take(k, 1))

    def activate(k):
        gate = part[k, 0, dp] + take(k, 2) + take(k, 5)
        up = part[k, 1, dp] + take(k, 3) + take(k, 4)
        hid[k, dp] = (gate / (1.0 + jnp.exp(-gate)) * up).astype(BF16)
        for r in (1, 2):
            hid_copies[k, r - 1] = send(
                hid.at[k, dp], hid.at[k, dp],
                hid_send.at[k, r - 1], hid_recv.at[k, r - 1], {"dp": dx[r]},
            )

    def hand_on(k):
        cut = ffw // 256 * 128
        for r, first, size in ((1, 0, cut), (2, cut, ffw - cut)):
            hid_copies[k, r - 1].wait_recv()
            piece = hid.at[k, dx[r], :, pl.ds(first, size)]
            hid_copies[k, r + 1] = send(
                piece, piece, hid_send.at[k, r + 1], hid_recv.at[k, r + 1], {"dp": dx[3 - r]},
            )

    pair_copies, z_copies = {}, {}

    def down_side(k):
        hid_copies[k, 2].wait_recv()
        hid_copies[k, 3].wait_recv()
        table = mix[zx[k]]
        name = lax.broadcasted_iota(jnp.int32, table.shape, 1)
        spread = (2, rows, rows)
        same = lax.broadcasted_iota(jnp.int32, spread, 1) == lax.broadcasted_iota(jnp.int32, spread, 2)
        acc = None
        for e in range(local):
            ready(e, 2)
            row = jnp.sum(jnp.where(name == me * local + e, table, 0.0), axis=1, keepdims=True)
            share = jnp.sum(jnp.where(same, row, 0.0), axis=2, keepdims=True)
            o = jnp.dot(rows_of(hid[k, 2 * e : 2 * e + 2]), wd[e], preferred_element_type=F32)
            o = share * o.reshape(2, rows, o.shape[1])
            acc = o if acc is None else acc + o
        outp[k] = acc
        pout[k] = outp[k, other].astype(BF16)
        pair_copies[k] = send(
            pout.at[k], pair.at[k], pair_send.at[k], pair_recv.at[k], partner
        )

    def both(k):
        pair_copies[k].wait_recv()
        return outp[k, core] + pair[k].astype(F32)

    def ship(k):
        zsend[k - 1] = both(k).astype(BF16)
        z_copies[k] = send(
            zsend.at[k - 1], zgot.at[k - 1], z_send.at[k - 1], z_recv.at[k - 1],
            {"expert": zx[k] * 2 + core},
        )

    up_side(0)
    pass_on(2)
    relay(0)
    pass_on(3)
    up_side(2)
    pass_on(1)
    up_side(3)
    relay(2)
    activate(0)
    up_side(1)
    relay(3)
    activate(2)
    hand_on(0)
    relay(1)
    activate(3)
    hand_on(2)
    for k in (2, 3, 1):
        pass_mix(k)
    activate(1)
    hand_on(3)
    for k in range(4):
        mix_fwd[k].wait_recv()
    down_side(2)
    down_side(0)
    hand_on(1)
    ship(2)
    down_side(3)
    ship(3)
    total = both(0)
    down_side(1)
    ship(1)
    for k in (2, 3, 1):
        z_copies[k].wait_recv()
        total = total + zgot[k - 1].astype(F32)
    out_ref[...] = total.astype(BF16)
    for copy in sent:
        copy.wait_send()


def dense_shards(tokens, expert_ids, router_probs, w_gate, w_up, w_down):
    rows, width = tokens.shape
    local, _, ffw = w_gate.shape
    if local != 2:
        return shards(tokens, expert_ids, router_probs, w_gate, w_up, w_down)
    vmem, dma = pltpu.VMEM, pltpu.SemaphoreType.DMA
    in_place = pl.BlockSpec(memory_space=pl.ANY)
    return pl.pallas_call(
        kernel,
        out_shape=pltpu.VMEM((rows, width), BF16),
        in_specs=[in_place] * 6,
        out_specs=pl.BlockSpec(memory_space=pltpu.VMEM),
        scratch_shapes=[
            vmem((rows, width), BF16),
            vmem(expert_ids.shape[::-1], jnp.int32),
            vmem(expert_ids.shape[::-1], F32),
            vmem((local, width, ffw), BF16),
            vmem((local, width, ffw), BF16),
            vmem((local, ffw, width), BF16),
            vmem((4, 2, rows, width), BF16),
            vmem((4, 2, 8 * local, rows), F32),
            vmem((4, 2, 4, rows, ffw), F32),
            vmem((4, 6, rows, ffw), BF16),
            vmem((4, 6, rows, ffw), BF16),
            vmem((4, 4, rows, ffw), BF16),
            vmem((4, 2, rows, width), F32),
            vmem((4, rows, width), BF16),
            vmem((4, rows, width), BF16),
            vmem((3, rows, width), BF16),
            vmem((3, rows, width), BF16),
            dma((3,)),
            dma((3 * local,)),
            dma((3,)), dma((3,)),
            dma((4,)), dma((4,)),
            dma((3,)), dma((3,)),
            dma((4,)), dma((4,)),
            dma((4, 6)), dma((4, 6)),
            dma((4, 4)), dma((4, 4)),
            dma((4,)), dma((4,)),
            dma((3,)), dma((3,)),
        ],
        compiler_params=pltpu.CompilerParams(
            collective_id=0, has_side_effects=True, vmem_limit_bytes=65_000_000
        ),
    )(tokens, expert_ids.T, router_probs.T, w_gate, w_up, w_down)


def solution(mesh):
    in_specs = (
        P("expert", "dp"),
        P("expert", None),
        P("expert", None),
        P("expert", "dp", None),
        P("expert", "dp", None),
        P("expert", None, "dp"),
    )
    out_specs = P("expert", "dp")
    dense = mesh.shape["dp"] == 4 and mesh.shape["expert"] == 8
    body = dense_shards if dense else shards
    return jax.shard_map(body, mesh=mesh, in_specs=in_specs, out_specs=out_specs, check_vma=False)
```

```python
import functools

import jax
import jax.numpy as jnp
from jax import lax
from jax.experimental import pallas as pl
from jax.experimental.pallas import tpu as pltpu
from jax.sharding import PartitionSpec as P

MESH = pl.DeviceIdType.MESH
F32, BF16 = jnp.float32, jnp.bfloat16


def from_root(x, axis, root):
    mine = lax.axis_index(axis) == root
    return lax.psum(jnp.where(mine, x, jnp.zeros_like(x)), axis)


def shards(tokens, expert_ids, router_probs, w_gate, w_up, w_down):
    tok_rows, width_part = tokens.shape
    top_count = expert_ids.shape[1]
    local_experts = w_gate.shape[0]
    groups = lax.axis_size("expert")
    experts_all = local_experts * groups
    capacity = max(2, (tok_rows * top_count + experts_all - 4) // (experts_all - 3))
    slots_all = experts_all * capacity
    weights = router_probs / jnp.sum(router_probs, axis=1, keepdims=True)
    flat_ids = expert_ids.reshape(-1)
    every_expert = jnp.arange(experts_all, dtype=jnp.int32)
    named_table = (flat_ids[:, None] == every_expert[None, :]).astype(jnp.int32)
    local_counts = jnp.sum(named_table, axis=0)
    above_cap = (local_counts > capacity).astype(jnp.int32)
    first_hot = jnp.argmax(above_cap)
    second_hot = experts_all - 1 - jnp.argmax(above_cap[::-1])
    hot_ids = jnp.stack([first_hot, second_hot])
    is_hot = (expert_ids == hot_ids[0]) | (expert_ids == hot_ids[1])
    cold_mask = jnp.logical_not(is_hot).reshape(-1)
    member = named_table * cold_mask[:, None].astype(jnp.int32)
    row = jnp.arange(member.shape[0], dtype=jnp.int32)
    before = (row[:, None] > row[None, :]).astype(jnp.bfloat16)
    earlier = jnp.dot(before, member.astype(jnp.bfloat16), preferred_element_type=jnp.float32)
    position = jnp.sum(earlier.astype(jnp.int32) * member, axis=1)
    slot_index = jnp.where(cold_mask, flat_ids * capacity + position, -1)
    matches = (slot_index[:, None] == jnp.arange(slots_all, dtype=jnp.int32)[None, :]).reshape(
        tok_rows, top_count, slots_all
    )
    chosen = jnp.sum(matches.astype(jnp.bfloat16), axis=1)
    combine_mat = jnp.sum(jnp.where(matches, weights[:, :, None], 0.0), axis=1)
    outgoing = jnp.einsum("ts,td->sd", chosen, tokens, preferred_element_type=jnp.float32).astype(
        jnp.bfloat16
    )
    outgoing = outgoing.reshape(groups, local_experts, capacity, width_part)
    received = lax.all_to_all(outgoing, "expert", split_axis=0, concat_axis=0, tiled=True)
    gate_part = jnp.einsum("secd,edf->escf", received, w_gate, preferred_element_type=jnp.float32)
    up_part = jnp.einsum("secd,edf->escf", received, w_up, preferred_element_type=jnp.float32)
    gate_sum, up_sum = lax.psum((gate_part, up_part), "dp")
    hidden = (jax.nn.silu(gate_sum) * up_sum).astype(jnp.bfloat16)
    output = jnp.einsum("escf,efd->secd", hidden, w_down, preferred_element_type=jnp.float32)
    results = output.astype(jnp.bfloat16)
    returned = lax.all_to_all(results, "expert", split_axis=0, concat_axis=0, tiled=True)
    main_part = jnp.dot(
        combine_mat,
        returned.reshape(slots_all, width_part).astype(jnp.float32),
        precision=lax.Precision.HIGHEST,
    )
    hot_gates = []
    hot_ups = []
    hot_downs = []
    for hot_slot in range(2):
        hot_expert = hot_ids[hot_slot]
        root_index = hot_expert // local_experts
        local_index = hot_expert % local_experts
        pieces = (
            lax.dynamic_index_in_dim(w_gate, local_index, 0, keepdims=False),
            lax.dynamic_index_in_dim(w_up, local_index, 0, keepdims=False),
            lax.dynamic_index_in_dim(w_down, local_index, 0, keepdims=False),
        )
        gate_copy, up_copy, down_copy = (
            from_root(pieces[0], "expert", root_index),
            from_root(pieces[1], "expert", root_index),
            from_root(pieces[2], "expert", root_index),
        )
        hot_gates.append(jnp.dot(tokens, gate_copy, preferred_element_type=jnp.float32))
        hot_ups.append(jnp.dot(tokens, up_copy, preferred_element_type=jnp.float32))
        hot_downs.append(down_copy)
    gate_total, up_total = lax.psum((jnp.stack(hot_gates), jnp.stack(hot_ups)), "dp")
    hot_hidden = (jax.nn.silu(gate_total) * up_total).astype(jnp.bfloat16)
    total = main_part
    for hot_slot in range(2):
        hot_out = jnp.dot(
            hot_hidden[hot_slot], hot_downs[hot_slot], preferred_element_type=jnp.float32
        ).astype(jnp.bfloat16)
        hot_weight = jnp.sum(jnp.where(expert_ids == hot_ids[hot_slot], weights, 0.0), axis=1)
        total = total + hot_weight[:, None] * hot_out.astype(jnp.float32)
    return total.astype(jnp.bfloat16)


def rows_of(blocks):
    count, rows, width = blocks.shape
    return blocks.astype(F32).reshape(count * rows, width).astype(BF16)


def kernel(
    tokens_hbm, ids_hbm, probs_hbm, gate_hbm, up_hbm, down_hbm, out_ref,
    ids_ref, probs_ref, wg, wu, wd, tok, mix, shares, part, leave, got, hid, outp, pout, pair, zsend, zgot,
    in_sem, w_sem, tok_send, tok_recv, fwd_send, fwd_recv, mix_send, mix_recv,
    part_send, part_recv, hid_send, hid_recv, pair_send, pair_recv, z_send, z_recv,
):
    local, _, ffw = wg.shape
    rows = tok.shape[2]
    dp = lax.axis_index("dp")
    me = lax.axis_index("expert")
    z, core = me // 2, me % 2
    low, high = z % 2, z // 2
    zx = (z, z + 1 - 2 * low, z + 2 - 4 * high, 3 - z)
    dlow, dhigh = dp % 2, dp // 2
    dx = (dp, dp + 1 - 2 * dlow, dp + 2 - 4 * dhigh, 3 - dp)
    other = 1 - core
    partner = {"expert": z * 2 + other}

    barrier = pltpu.get_barrier_semaphore()
    for k in (2, 3, 1):
        for c in (core, other):
            pl.semaphore_signal(barrier, inc=1, device_id={"expert": zx[k] * 2 + c}, device_id_type=MESH)
    for r in (3, 1, 2):
        pl.semaphore_signal(barrier, inc=1, device_id={"dp": dx[r]}, device_id_type=MESH)
    pl.semaphore_signal(barrier, inc=1, device_id=partner, device_id_type=MESH)

    sent = []

    def send(src, dst, s_sem, r_sem, device):
        copy = pltpu.make_async_remote_copy(
            src_ref=src, dst_ref=dst, send_sem=s_sem, recv_sem=r_sem,
            device_id=device, device_id_type=MESH,
        )
        copy.start()
        sent.append(copy)
        return copy

    small = [
        pltpu.make_async_copy(tokens_hbm, tok.at[z, core], in_sem.at[0]),
        pltpu.make_async_copy(ids_hbm, ids_ref, in_sem.at[1]),
        pltpu.make_async_copy(probs_hbm, probs_ref, in_sem.at[2]),
    ]
    for copy in small:
        copy.start()
    loads = []
    for e in range(local):
        loads.append([
            pltpu.make_async_copy(gate_hbm.at[e], wg.at[e], w_sem.at[3 * e]),
            pltpu.make_async_copy(up_hbm.at[e], wu.at[e], w_sem.at[3 * e + 1]),
            pltpu.make_async_copy(down_hbm.at[e], wd.at[e], w_sem.at[3 * e + 2]),
        ])
    for which in range(3):
        for e in range(local):
            loads[e][which].start()

    def ready(e, which):
        if loads[e][which] is not None:
            loads[e][which].wait()
            loads[e][which] = None

    small[0].wait()
    pl.semaphore_wait(barrier, 10)

    tok_copies, fwd_copies = {}, {}
    own = tok.at[z, core]
    fwd_copies[0] = send(own, own, fwd_send.at[0], fwd_recv.at[0], partner)
    tok_copies[2] = send(own, own, tok_send.at[1], tok_recv.at[1], {'expert': zx[2] * 2 + core})
    tok_copies[1] = send(own, own, tok_send.at[0], tok_recv.at[0], {'expert': zx[1] * 2 + core})
    tok_copies[3] = send(own, own, tok_send.at[2], tok_recv.at[2], {'expert': zx[3] * 2 + core})

    mix_copies = []

    def route():
        small[1].wait()
        small[2].wait()
        probs = probs_ref[...]
        weights = probs / jnp.sum(probs, axis=0, keepdims=True)
        ids = ids_ref[...]
        named = lax.broadcasted_iota(jnp.int32, mix.shape[2:], 0)
        table = jnp.zeros(mix.shape[2:], F32)
        for k in range(ids.shape[0]):
            table = table + jnp.where(ids[k : k + 1] == named, weights[k : k + 1], 0.0)
        mix[z, core] = table
        mine = mix.at[z, core]
        mix_copies.append(send(mine, mine, mix_send.at[0], mix_recv.at[0], partner))
        for k in range(1, 4):
            for flip, c in enumerate((core, other)):
                mix_copies.append(send(
                    mine, mine, mix_send.at[2 * k - 1 + flip], mix_recv.at[2 * k - 1 + flip],
                    {"expert": zx[k] * 2 + c},
                ))

    def pass_on(k):
        tok_copies[k].wait_recv()
        here = tok.at[zx[k], core]
        fwd_copies[k] = send(here, here, fwd_send.at[k], fwd_recv.at[k], partner)

    part_copies, hid_copies = {}, {}

    def put(k, slot, device):
        part_copies[k, slot] = send(
            leave.at[k, slot], got.at[k, slot], part_send.at[k, slot], part_recv.at[k, slot], device,
        )

    def take(k, slot):
        part_copies[k, slot].wait_recv()
        return got[k, slot].astype(F32)

    def half(k, which, w):
        x = rows_of(tok[zx[k]])
        for e in range(local):
            ready(e, which)
            part[k, which, 2 * e : 2 * e + 2] = (
                jnp.dot(x, w[e], preferred_element_type=F32).reshape(2, rows, ffw)
            )
        if k in (1, 3):
            for slot, r in ((which, 3), (2 + which, 1 + which)):
                leave[k, slot] = part[k, which, dx[r]].astype(BF16)
                put(k, slot, {"dp": dx[1 + which]})
        else:
            for r in (3, 1, 2):
                leave[k, 2 * r - 2 + which] = part[k, which, dx[r]].astype(BF16)
                put(k, 2 * r - 2 + which, {"dp": dx[r]})

    def gate_side(k):
        fwd_copies[k].wait_recv()
        half(k, 0, wg)

    def up_side(k):
        half(k, 1, wu)

    def relay_gate(k):
        leave[k, 5] = (part[k, 0, dx[2]] + take(k, 0)).astype(BF16)
        put(k, 5, {"dp": dx[2]})

    def relay_up(k):
        leave[k, 4] = (part[k, 1, dx[1]] + take(k, 1)).astype(BF16)
        put(k, 4, {"dp": dx[1]})

    def activate(k):
        if k in (1, 3):
            gate = part[k, 0, dp] + take(k, 2) + take(k, 5)
            up = part[k, 1, dp] + take(k, 3) + take(k, 4)
        else:
            gate = part[k, 0, dp] + take(k, 0) + take(k, 2) + take(k, 4)
            up = part[k, 1, dp] + take(k, 1) + take(k, 3) + take(k, 5)
        hid[k, dp] = (gate / (1.0 + jnp.exp(-gate)) * up).astype(BF16)
        for r in (1, 2) if k in (0, 2) else (3, 1, 2):
            hid_copies[k, r] = send(
                hid.at[k, dp], hid.at[k, dp],
                hid_send.at[k, r], hid_recv.at[k, r], {"dp": dx[r]},
            )

    def hand_on(k):
        cut = ffw // 256 * 128
        for r, first, size, slot in ((1, 0, cut, 3), (2, cut, ffw - cut, 0)):
            hid_copies[k, r].wait_recv()
            piece = hid.at[k, dx[r], :, pl.ds(first, size)]
            hid_copies[k, slot] = send(
                piece, piece, hid_send.at[k, slot], hid_recv.at[k, slot], {"dp": dx[3 - r]},
            )

    pair_copies, z_copies = {}, {}

    def down_side(k):
        for r in (3, 0) if k in (0, 2) else (1, 2, 3):
            hid_copies[k, r].wait_recv()
        acc = None
        for e in range(local):
            ready(e, 2)
            o = jnp.dot(rows_of(hid[k, 2 * e : 2 * e + 2]), wd[e], preferred_element_type=F32)
            o = jnp.tile(shares[k, e], (1, 1, o.shape[1] // 128)) * o.reshape(2, rows, o.shape[1])
            acc = o if acc is None else acc + o
        outp[k] = acc
        pout[k] = outp[k, other].astype(BF16)
        pair_copies[k] = send(
            pout.at[k], pair.at[k], pair_send.at[k], pair_recv.at[k], partner
        )

    def both(k):
        pair_copies[k].wait_recv()
        return outp[k, core] + pair[k].astype(F32)

    def ship(k):
        zsend[k - 1] = both(k).astype(BF16)
        z_copies[k] = send(
            zsend.at[k - 1], zgot.at[k - 1], z_send.at[k - 1], z_recv.at[k - 1],
            {"expert": zx[k] * 2 + core},
        )

    def mixed():
        for copy in mix_copies:
            copy.wait_recv()
        spread = (2, rows, rows)
        same = lax.broadcasted_iota(jnp.int32, spread, 1) == lax.broadcasted_iota(jnp.int32, spread, 2)
        for k in range(4):
            table = mix[zx[k]]
            name = lax.broadcasted_iota(jnp.int32, table.shape, 1)
            for e in range(local):
                row = jnp.sum(jnp.where(name == me * local + e, table, 0.0), axis=1, keepdims=True)
                share = jnp.sum(jnp.where(same, row, 0.0), axis=2, keepdims=True)
                shares[k, e] = jnp.broadcast_to(share, shares.shape[2:])

    gate_side(0)
    up_side(0)
    route()
    pass_on(2)
    gate_side(2)
    pass_on(3)
    up_side(2)
    gate_side(3)
    pass_on(1)
    up_side(3)
    mixed()
    gate_side(1)
    activate(2)
    up_side(1)
    relay_gate(3)
    activate(0)
    relay_up(3)
    hand_on(2)
    relay_gate(1)
    relay_up(1)
    activate(3)
    down_side(2)
    activate(1)
    ship(2)
    hand_on(0)
    down_side(3)
    ship(3)
    down_side(1)
    ship(1)
    down_side(0)
    total = both(0)
    for k in (3, 2, 1):
        z_copies[k].wait_recv()
        total = total + zgot[k - 1].astype(F32)
    out_ref[...] = total.astype(BF16)
    for copy in sent:
        copy.wait_send()


def dense_shards(tokens, expert_ids, router_probs, w_gate, w_up, w_down):
    rows, width = tokens.shape
    local, _, ffw = w_gate.shape
    if local != 2:
        return shards(tokens, expert_ids, router_probs, w_gate, w_up, w_down)
    vmem, dma = pltpu.VMEM, pltpu.SemaphoreType.DMA
    in_place = pl.BlockSpec(memory_space=pl.ANY)
    return pl.pallas_call(
        kernel,
        out_shape=pltpu.VMEM((rows, width), BF16),
        in_specs=[in_place] * 6,
        out_specs=pl.BlockSpec(memory_space=pltpu.VMEM),
        scratch_shapes=[
            vmem(expert_ids.shape[::-1], jnp.int32),
            vmem(expert_ids.shape[::-1], F32),
            vmem((local, width, ffw), BF16),
            vmem((local, width, ffw), BF16),
            vmem((local, ffw, width), BF16),
            vmem((4, 2, rows, width), BF16),
            vmem((4, 2, 8 * local, rows), F32),
            vmem((4, local, 2, rows, 128), F32),
            vmem((4, 2, 4, rows, ffw), F32),
            vmem((4, 6, rows, ffw), BF16),
            vmem((4, 6, rows, ffw), BF16),
            vmem((4, 4, rows, ffw), BF16),
            vmem((4, 2, rows, width), F32),
            vmem((4, rows, width), BF16),
            vmem((4, rows, width), BF16),
            vmem((3, rows, width), BF16),
            vmem((3, rows, width), BF16),
            dma((3,)),
            dma((3 * local,)),
            dma((3,)), dma((3,)),
            dma((4,)), dma((4,)),
            dma((7,)), dma((7,)),
            dma((4, 6)), dma((4, 6)),
            dma((4, 4)), dma((4, 4)),
            dma((4,)), dma((4,)),
            dma((3,)), dma((3,)),
        ],
        compiler_params=pltpu.CompilerParams(
            collective_id=0, has_side_effects=True, vmem_limit_bytes=65_000_000
        ),
    )(tokens, expert_ids.T, router_probs.T, w_gate, w_up, w_down)


def solution(mesh):
    in_specs = (
        P("expert", "dp"),
        P("expert", None),
        P("expert", None),
        P("expert", "dp", None),
        P("expert", "dp", None),
        P("expert", None, "dp"),
    )
    out_specs = P("expert", "dp")
    dense = mesh.shape["dp"] == 4 and mesh.shape["expert"] == 8
    body = dense_shards if dense else shards
    return jax.shard_map(body, mesh=mesh, in_specs=in_specs, out_specs=out_specs, check_vma=False)
```

```python
import functools

import jax
import jax.numpy as jnp
from jax import lax
from jax.experimental import pallas as pl
from jax.experimental.pallas import tpu as pltpu
from jax.sharding import PartitionSpec as P

MESH = pl.DeviceIdType.MESH
F32, BF16 = jnp.float32, jnp.bfloat16


def from_root(x, axis, root):
    mine = lax.axis_index(axis) == root
    return lax.psum(jnp.where(mine, x, jnp.zeros_like(x)), axis)


def shards(tokens, expert_ids, router_probs, w_gate, w_up, w_down):
    tok_rows, width_part = tokens.shape
    top_count = expert_ids.shape[1]
    local_experts = w_gate.shape[0]
    groups = lax.axis_size("expert")
    experts_all = local_experts * groups
    capacity = max(2, (tok_rows * top_count + experts_all - 4) // (experts_all - 3))
    slots_all = experts_all * capacity
    weights = router_probs / jnp.sum(router_probs, axis=1, keepdims=True)
    flat_ids = expert_ids.reshape(-1)
    every_expert = jnp.arange(experts_all, dtype=jnp.int32)
    named_table = (flat_ids[:, None] == every_expert[None, :]).astype(jnp.int32)
    local_counts = jnp.sum(named_table, axis=0)
    above_cap = (local_counts > capacity).astype(jnp.int32)
    first_hot = jnp.argmax(above_cap)
    second_hot = experts_all - 1 - jnp.argmax(above_cap[::-1])
    hot_ids = jnp.stack([first_hot, second_hot])
    is_hot = (expert_ids == hot_ids[0]) | (expert_ids == hot_ids[1])
    cold_mask = jnp.logical_not(is_hot).reshape(-1)
    member = named_table * cold_mask[:, None].astype(jnp.int32)
    row = jnp.arange(member.shape[0], dtype=jnp.int32)
    before = (row[:, None] > row[None, :]).astype(jnp.bfloat16)
    earlier = jnp.dot(before, member.astype(jnp.bfloat16), preferred_element_type=jnp.float32)
    position = jnp.sum(earlier.astype(jnp.int32) * member, axis=1)
    slot_index = jnp.where(cold_mask, flat_ids * capacity + position, -1)
    matches = (slot_index[:, None] == jnp.arange(slots_all, dtype=jnp.int32)[None, :]).reshape(
        tok_rows, top_count, slots_all
    )
    chosen = jnp.sum(matches.astype(jnp.bfloat16), axis=1)
    combine_mat = jnp.sum(jnp.where(matches, weights[:, :, None], 0.0), axis=1)
    outgoing = jnp.einsum("ts,td->sd", chosen, tokens, preferred_element_type=jnp.float32).astype(
        jnp.bfloat16
    )
    outgoing = outgoing.reshape(groups, local_experts, capacity, width_part)
    received = lax.all_to_all(outgoing, "expert", split_axis=0, concat_axis=0, tiled=True)
    gate_part = jnp.einsum("secd,edf->escf", received, w_gate, preferred_element_type=jnp.float32)
    up_part = jnp.einsum("secd,edf->escf", received, w_up, preferred_element_type=jnp.float32)
    gate_sum, up_sum = lax.psum((gate_part, up_part), "dp")
    hidden = (jax.nn.silu(gate_sum) * up_sum).astype(jnp.bfloat16)
    output = jnp.einsum("escf,efd->secd", hidden, w_down, preferred_element_type=jnp.float32)
    results = output.astype(jnp.bfloat16)
    returned = lax.all_to_all(results, "expert", split_axis=0, concat_axis=0, tiled=True)
    main_part = jnp.dot(
        combine_mat,
        returned.reshape(slots_all, width_part).astype(jnp.float32),
        precision=lax.Precision.HIGHEST,
    )
    hot_gates = []
    hot_ups = []
    hot_downs = []
    for hot_slot in range(2):
        hot_expert = hot_ids[hot_slot]
        root_index = hot_expert // local_experts
        local_index = hot_expert % local_experts
        pieces = (
            lax.dynamic_index_in_dim(w_gate, local_index, 0, keepdims=False),
            lax.dynamic_index_in_dim(w_up, local_index, 0, keepdims=False),
            lax.dynamic_index_in_dim(w_down, local_index, 0, keepdims=False),
        )
        gate_copy, up_copy, down_copy = (
            from_root(pieces[0], "expert", root_index),
            from_root(pieces[1], "expert", root_index),
            from_root(pieces[2], "expert", root_index),
        )
        hot_gates.append(jnp.dot(tokens, gate_copy, preferred_element_type=jnp.float32))
        hot_ups.append(jnp.dot(tokens, up_copy, preferred_element_type=jnp.float32))
        hot_downs.append(down_copy)
    gate_total, up_total = lax.psum((jnp.stack(hot_gates), jnp.stack(hot_ups)), "dp")
    hot_hidden = (jax.nn.silu(gate_total) * up_total).astype(jnp.bfloat16)
    total = main_part
    for hot_slot in range(2):
        hot_out = jnp.dot(
            hot_hidden[hot_slot], hot_downs[hot_slot], preferred_element_type=jnp.float32
        ).astype(jnp.bfloat16)
        hot_weight = jnp.sum(jnp.where(expert_ids == hot_ids[hot_slot], weights, 0.0), axis=1)
        total = total + hot_weight[:, None] * hot_out.astype(jnp.float32)
    return total.astype(jnp.bfloat16)


def rows_of(blocks):
    count, rows, width = blocks.shape
    return blocks.astype(F32).reshape(count * rows, width).astype(BF16)


def kernel(
    tokens_hbm, ids_hbm, probs_hbm, gate_hbm, up_hbm, down_hbm, out_ref,
    ids_ref, probs_ref, wg, wu, wd, tok, mix, shares, part, leave, got, hid, outp, pout, pair, zsend, zgot,
    in_sem, w_sem, tok_send, tok_recv, fwd_send, fwd_recv, mix_send, mix_recv,
    part_send, part_recv, hid_send, hid_recv, pair_send, pair_recv, z_send, z_recv,
):
    local, _, ffw = wg.shape
    rows = tok.shape[2]
    dp = lax.axis_index("dp")
    me = lax.axis_index("expert")
    z, core = me // 2, me % 2
    low, high = z % 2, z // 2
    zx = (z, z + 1 - 2 * low, z + 2 - 4 * high, 3 - z)
    dlow, dhigh = dp % 2, dp // 2
    dx = (dp, dp + 1 - 2 * dlow, dp + 2 - 4 * dhigh, 3 - dp)
    other = 1 - core
    partner = {"expert": z * 2 + other}

    barrier = pltpu.get_barrier_semaphore()
    for k in (2, 3, 1):
        for c in (core, other):
            pl.semaphore_signal(barrier, inc=1, device_id={"expert": zx[k] * 2 + c}, device_id_type=MESH)
    for r in (3, 1, 2):
        pl.semaphore_signal(barrier, inc=1, device_id={"dp": dx[r]}, device_id_type=MESH)
    pl.semaphore_signal(barrier, inc=1, device_id=partner, device_id_type=MESH)

    sent = []

    def send(src, dst, s_sem, r_sem, device):
        copy = pltpu.make_async_remote_copy(
            src_ref=src, dst_ref=dst, send_sem=s_sem, recv_sem=r_sem,
            device_id=device, device_id_type=MESH,
        )
        copy.start()
        sent.append(copy)
        return copy

    small = [
        pltpu.make_async_copy(tokens_hbm, tok.at[z, core], in_sem.at[0]),
        pltpu.make_async_copy(ids_hbm, ids_ref, in_sem.at[1]),
        pltpu.make_async_copy(probs_hbm, probs_ref, in_sem.at[2]),
    ]
    for copy in small:
        copy.start()
    loads = []
    for e in range(local):
        loads.append([
            pltpu.make_async_copy(gate_hbm.at[e], wg.at[e], w_sem.at[3 * e]),
            pltpu.make_async_copy(up_hbm.at[e], wu.at[e], w_sem.at[3 * e + 1]),
            pltpu.make_async_copy(down_hbm.at[e], wd.at[e], w_sem.at[3 * e + 2]),
        ])
    for which in range(3):
        for e in range(local):
            loads[e][which].start()

    def ready(e, which):
        if loads[e][which] is not None:
            loads[e][which].wait()
            loads[e][which] = None

    small[0].wait()
    pl.semaphore_wait(barrier, 10)

    tok_copies, fwd_copies = {}, {}
    own = tok.at[z, core]
    fwd_copies[0] = send(own, own, fwd_send.at[0], fwd_recv.at[0], partner)
    tok_copies[2] = send(own, own, tok_send.at[1], tok_recv.at[1], {'expert': zx[2] * 2 + core})
    tok_copies[1] = send(own, own, tok_send.at[0], tok_recv.at[0], {'expert': zx[1] * 2 + core})
    tok_copies[3] = send(own, own, tok_send.at[2], tok_recv.at[2], {'expert': zx[3] * 2 + core})

    mix_copies = []

    def route():
        small[1].wait()
        small[2].wait()
        probs = probs_ref[...]
        weights = probs / jnp.sum(probs, axis=0, keepdims=True)
        ids = ids_ref[...]
        named = lax.broadcasted_iota(jnp.int32, mix.shape[2:], 0)
        table = jnp.zeros(mix.shape[2:], F32)
        for k in range(ids.shape[0]):
            table = table + jnp.where(ids[k : k + 1] == named, weights[k : k + 1], 0.0)
        mix[z, core] = table
        mine = mix.at[z, core]
        mix_copies.append(send(mine, mine, mix_send.at[0], mix_recv.at[0], partner))
        for k in range(1, 4):
            for flip, c in enumerate((core, other)):
                mix_copies.append(send(
                    mine, mine, mix_send.at[2 * k - 1 + flip], mix_recv.at[2 * k - 1 + flip],
                    {"expert": zx[k] * 2 + c},
                ))

    def pass_on(k):
        tok_copies[k].wait_recv()
        here = tok.at[zx[k], core]
        fwd_copies[k] = send(here, here, fwd_send.at[k], fwd_recv.at[k], partner)

    part_copies, hid_copies = {}, {}

    def put(k, slot, device):
        part_copies[k, slot] = send(
            leave.at[k, slot], got.at[k, slot], part_send.at[k, slot], part_recv.at[k, slot], device,
        )

    def take(k, slot):
        part_copies[k, slot].wait_recv()
        return got[k, slot].astype(F32)

    def half(k, which, w):
        x = rows_of(tok[zx[k]])
        for e in range(local):
            ready(e, which)
            part[k, which, 2 * e : 2 * e + 2] = (
                jnp.dot(x, w[e], preferred_element_type=F32).reshape(2, rows, ffw)
            )
        if k in (1, 3):
            for slot, r in ((which, 3), (2 + which, 1 + which)):
                leave[k, slot] = part[k, which, dx[r]].astype(BF16)
                put(k, slot, {"dp": dx[1 + which]})
        else:
            for r in (3, 1, 2):
                leave[k, 2 * r - 2 + which] = part[k, which, dx[r]].astype(BF16)
                put(k, 2 * r - 2 + which, {"dp": dx[r]})

    def gate_side(k):
        fwd_copies[k].wait_recv()
        half(k, 0, wg)

    def up_side(k):
        half(k, 1, wu)

    def relay_gate(k):
        leave[k, 5] = (part[k, 0, dx[2]] + take(k, 0)).astype(BF16)
        put(k, 5, {"dp": dx[2]})

    def relay_up(k):
        leave[k, 4] = (part[k, 1, dx[1]] + take(k, 1)).astype(BF16)
        put(k, 4, {"dp": dx[1]})

    def activate(k):
        if k in (1, 3):
            gate = part[k, 0, dp] + take(k, 2) + take(k, 5)
            up = part[k, 1, dp] + take(k, 3) + take(k, 4)
        else:
            gate = part[k, 0, dp] + take(k, 0) + take(k, 2) + take(k, 4)
            up = part[k, 1, dp] + take(k, 1) + take(k, 3) + take(k, 5)
        hid[k, dp] = (gate / (1.0 + jnp.exp(-gate)) * up).astype(BF16)
        for r in (1, 2) if k in (0, 2) else (3, 1, 2):
            hid_copies[k, r] = send(
                hid.at[k, dp], hid.at[k, dp],
                hid_send.at[k, r], hid_recv.at[k, r], {"dp": dx[r]},
            )

    def hand_on(k):
        cut = ffw // 256 * 128
        for r, first, size, slot in ((1, 0, cut, 3), (2, cut, ffw - cut, 0)):
            hid_copies[k, r].wait_recv()
            piece = hid.at[k, dx[r], :, pl.ds(first, size)]
            hid_copies[k, slot] = send(
                piece, piece, hid_send.at[k, slot], hid_recv.at[k, slot], {"dp": dx[3 - r]},
            )

    pair_copies, z_copies = {}, {}

    def down_side(k):
        for r in (3, 0) if k in (0, 2) else (1, 2, 3):
            hid_copies[k, r].wait_recv()
        acc = None
        for e in range(local):
            ready(e, 2)
            o = jnp.dot(rows_of(hid[k, 2 * e : 2 * e + 2]), wd[e], preferred_element_type=F32)
            o = jnp.tile(shares[k, e], (1, 1, o.shape[1] // 128)) * o.reshape(2, rows, o.shape[1])
            acc = o if acc is None else acc + o
        outp[k] = acc
        pout[k] = outp[k, other].astype(BF16)
        pair_copies[k] = send(
            pout.at[k], pair.at[k], pair_send.at[k], pair_recv.at[k], partner
        )

    def both(k):
        pair_copies[k].wait_recv()
        return outp[k, core] + pair[k].astype(F32)

    def ship(k):
        zsend[k - 1] = both(k).astype(BF16)
        z_copies[k] = send(
            zsend.at[k - 1], zgot.at[k - 1], z_send.at[k - 1], z_recv.at[k - 1],
            {"expert": zx[k] * 2 + core},
        )

    def mixed():
        for copy in mix_copies:
            copy.wait_recv()
        spread = (2, rows, rows)
        same = lax.broadcasted_iota(jnp.int32, spread, 1) == lax.broadcasted_iota(jnp.int32, spread, 2)
        for k in range(4):
            table = mix[zx[k]]
            name = lax.broadcasted_iota(jnp.int32, table.shape, 1)
            for e in range(local):
                row = jnp.sum(jnp.where(name == me * local + e, table, 0.0), axis=1, keepdims=True)
                share = jnp.sum(jnp.where(same, row, 0.0), axis=2, keepdims=True)
                shares[k, e] = jnp.broadcast_to(share, shares.shape[2:])

    gate_side(0)
    up_side(0)
    route()
    pass_on(2)
    gate_side(2)
    pass_on(3)
    up_side(2)
    gate_side(3)
    pass_on(1)
    up_side(3)
    mixed()
    gate_side(1)
    activate(2)
    up_side(1)
    relay_gate(3)
    activate(0)
    relay_up(3)
    hand_on(2)
    relay_gate(1)
    relay_up(1)
    activate(3)
    down_side(2)
    activate(1)
    ship(2)
    hand_on(0)
    down_side(3)
    ship(3)
    down_side(1)
    ship(1)
    down_side(0)
    for copy in sent[:-2]:
        copy.wait_send()
    total = both(0)
    for k in (3, 2, 1):
        z_copies[k].wait_recv()
        total = total + zgot[k - 1].astype(F32)
    out_ref[...] = total.astype(BF16)
    for copy in sent[-2:]:
        copy.wait_send()


def dense_shards(tokens, expert_ids, router_probs, w_gate, w_up, w_down):
    rows, width = tokens.shape
    local, _, ffw = w_gate.shape
    if local != 2:
        return shards(tokens, expert_ids, router_probs, w_gate, w_up, w_down)
    vmem, dma = pltpu.VMEM, pltpu.SemaphoreType.DMA
    in_place = pl.BlockSpec(memory_space=pl.ANY)
    return pl.pallas_call(
        kernel,
        out_shape=pltpu.VMEM((rows, width), BF16),
        in_specs=[in_place] * 6,
        out_specs=pl.BlockSpec(memory_space=pltpu.VMEM),
        scratch_shapes=[
            vmem(expert_ids.shape[::-1], jnp.int32),
            vmem(expert_ids.shape[::-1], F32),
            vmem((local, width, ffw), BF16),
            vmem((local, width, ffw), BF16),
            vmem((local, ffw, width), BF16),
            vmem((4, 2, rows, width), BF16),
            vmem((4, 2, 8 * local, rows), F32),
            vmem((4, local, 2, rows, 128), F32),
            vmem((4, 2, 4, rows, ffw), F32),
            vmem((4, 6, rows, ffw), BF16),
            vmem((4, 6, rows, ffw), BF16),
            vmem((4, 4, rows, ffw), BF16),
            vmem((4, 2, rows, width), F32),
            vmem((4, rows, width), BF16),
            vmem((4, rows, width), BF16),
            vmem((3, rows, width), BF16),
            vmem((3, rows, width), BF16),
            dma((3,)),
            dma((3 * local,)),
            dma((3,)), dma((3,)),
            dma((4,)), dma((4,)),
            dma((7,)), dma((7,)),
            dma((4, 6)), dma((4, 6)),
            dma((4, 4)), dma((4, 4)),
            dma((4,)), dma((4,)),
            dma((3,)), dma((3,)),
        ],
        compiler_params=pltpu.CompilerParams(
            collective_id=0, has_side_effects=True, vmem_limit_bytes=65_000_000
        ),
    )(tokens, expert_ids.T, router_probs.T, w_gate, w_up, w_down)


def solution(mesh):
    in_specs = (
        P("expert", "dp"),
        P("expert", None),
        P("expert", None),
        P("expert", "dp", None),
        P("expert", "dp", None),
        P("expert", None, "dp"),
    )
    out_specs = P("expert", "dp")
    dense = mesh.shape["dp"] == 4 and mesh.shape["expert"] == 8
    body = dense_shards if dense else shards
    return jax.shard_map(body, mesh=mesh, in_specs=in_specs, out_specs=out_specs, check_vma=False)
```
